128 devices in a mesh: expert: 64 (over x, y_lo, z, core), hidden: 2 (over y_hi).
Axes of the slice: x: 4, y: 4 (y_hi: 2, y_lo: 2; y = y_hi * 2 + y_lo), z: 4, core: 2. Of those that a mesh axis runs over, the one named last changes fastest.
Arguments:
- tokens: bfloat16 [256, 256, 1024], P(('expert', 'hidden')), may hold values from -24 to 24
- router: bfloat16 [1024, 256], replicated, may hold values from -2 to 2
- out_grad: bfloat16 [256, 256, 1024], P(('expert', 'hidden')), may hold values from -24 to 24
- slot_outputs: bfloat16 [256, 256, 1024], P(('expert', 'hidden')), may hold values from -6 to 6
- preact: bfloat16 [128, 512, 4096], P('expert', None, 'hidden'), may hold values from -6 to 6
- w_in: bfloat16 [128, 1024, 4096], P('expert', None, 'hidden'), may hold values from -0.1875 to 0.1875
- w_out: bfloat16 [128, 4096, 1024], P('expert', 'hidden'), may hold values from -0.09375 to 0.09375
Outputs:
- grad_tokens: bfloat16 [256, 256, 1024], P(('expert', 'hidden'))
- grad_router: float32 [1024, 256], P(('expert', 'hidden'))
The draws below stay inside these ranges and needn't reach their ends.
All inputs are finite; a program needn't handle non-finite values.
Results may differ from the reference program's by a relative error of at most 0.017.
Values may be sent and summed in bfloat16 or wider, within the bound.
No kernel may reach another device: no remote copies, remote signals or barrier semaphores. Data moves between devices by JAX's collectives and lax.ppermute only.
A program may use at most 128 MiB of HBM per device.

```python
import jax
import jax.numpy as jnp
from jax import lax

D = 1024
HID = 4096
M = 256
SPE = 2
EXPERTS = 128
NS = 256
IMAGES = 256


router_scale = 0.09375


def draw_router(key, part):
    values = jax.random.normal(jax.random.fold_in(key, 5), (D, NS), jnp.float32)
    return (jnp.clip(values, -6.0, 6.0) * router_scale).astype(jnp.bfloat16)


def draw_tokens(key, part):
    values = jax.random.normal(jax.random.fold_in(key, 3), (IMAGES, M, D), jnp.float32)
    return jnp.clip(values, -6.0, 6.0).astype(jnp.bfloat16)


def block_scale(rng, dims, cuts, least, top_value):
    def one(axis_at, blocks):
        draws = jax.random.uniform(jax.random.fold_in(jax.random.fold_in(rng, 6), axis_at), (blocks,), jnp.float32, least / len(cuts), top_value / len(cuts))
        return jnp.repeat(jnp.exp(draws), dims[axis_at] // blocks).reshape((-1,) + (1,) * (len(dims) - axis_at - 1))

    gain = one(*cuts[0])
    for cut in cuts[1:]:
        gain = gain * one(*cut)
    return gain


def normal_values(rng, shape, deviation, limit, cuts=(), held_as=jnp.bfloat16):
    level = block_scale(rng, shape, cuts, -0.22, 0.18) if cuts else 1.0
    values = jax.random.normal(rng, shape, jnp.float32) * deviation * level
    return jnp.minimum(jnp.maximum(values, -limit), limit).astype(held_as)


def setup_inputs(seed: int = 0) -> dict:
    splits = jax.random.split(jax.random.key(seed), 8)
    return {
        "tokens": draw_tokens(jax.random.fold_in(splits[7], 71), 0),
        "router": draw_router(jax.random.fold_in(splits[7], 71), 0),
        "out_grad": normal_values(splits[2], (IMAGES, M, D), 4.0, 24.0, ((0, 128),)),
        "slot_outputs": normal_values(splits[3], (IMAGES, NS, D), 1.0, 6.0, ((0, 128),)),
        "preact": normal_values(splits[4], (EXPERTS, IMAGES * SPE, HID), 1.0, 6.0, ((0, 64), (2, 2))),
        "w_in": normal_values(splits[5], (EXPERTS, D, HID), D ** -0.5, 0.1875, ((0, 64), (2, 2))),
        "w_out": normal_values(splits[6], (EXPERTS, HID, D), HID ** -0.5, 0.09375, ((0, 64), (1, 2))),
    }


gelu_coef = 0.7978845608028654
cubic_coef = 0.044715


def gelu_slope(values):
    inner = gelu_coef * (values + cubic_coef * values * values * values)
    tanh_part = jnp.tanh(inner)
    return 0.5 * (1.0 + tanh_part) + 0.5 * values * (1.0 - tanh_part * tanh_part) * gelu_coef * (1.0 + 3.0 * cubic_coef * values * values)


def expert_back(pieces):
    grads, saved_pre, first_proj, second_proj = pieces
    grad_act = jnp.dot(grads, second_proj.T, preferred_element_type=jnp.float32)
    grad_pre = (grad_act * gelu_slope(saved_pre.astype(jnp.float32))).astype(jnp.bfloat16)
    return jnp.dot(grad_pre, first_proj.T, preferred_element_type=jnp.float32).astype(jnp.bfloat16)


def reference(tokens, router, out_grad, slot_outputs, preact, w_in, w_out):
    tok_f = tokens.astype(jnp.float32)
    grad_f = out_grad.astype(jnp.float32)
    router_f = router.astype(jnp.float32)
    logits = jnp.einsum("bmd,dn->bmn", tok_f, router_f)
    dispatch = jax.nn.softmax(logits, axis=1)
    combine = jax.nn.softmax(logits, axis=2)
    dispatch_b = dispatch.astype(jnp.bfloat16)
    combine_b = combine.astype(jnp.bfloat16)
    grad_combine = jnp.einsum("bmd,bnd->bmn", grad_f, slot_outputs.astype(jnp.float32))
    slot_grad = jnp.einsum("bmn,bmd->bnd", combine_b.astype(jnp.float32), grad_f).astype(jnp.bfloat16)
    grouped = slot_grad.reshape(IMAGES, EXPERTS, SPE, D).transpose(1, 0, 2, 3).reshape(EXPERTS, IMAGES * SPE, D)
    slot_in = lax.map(expert_back, (grouped, preact, w_in, w_out))
    slot_in_grad = slot_in.reshape(EXPERTS, IMAGES, SPE, D).transpose(1, 0, 2, 3).reshape(IMAGES, NS, D)
    slot_in_f = slot_in_grad.astype(jnp.float32)
    grad_dispatch = jnp.einsum("bmd,bnd->bmn", tok_f, slot_in_f)
    part_disp = dispatch * (grad_dispatch - jnp.sum(dispatch * grad_dispatch, axis=1, keepdims=True))
    part_comb = combine * (grad_combine - jnp.sum(combine * grad_combine, axis=2, keepdims=True))
    grad_logits = (part_disp + part_comb).astype(jnp.bfloat16)
    logit_f = grad_logits.astype(jnp.float32)
    grad_tokens = (jnp.einsum("bmn,bnd->bmd", dispatch_b.astype(jnp.float32), slot_in_f) + jnp.einsum("bmn,dn->bmd", logit_f, router_f)).astype(jnp.bfloat16)
    grad_router = jnp.einsum("bmd,bmn->dn", tok_f, logit_f) * (1.0 / IMAGES)
    return grad_tokens, grad_router
```

```python
import jax
import jax.numpy as jnp
from jax import lax
from jax.sharding import PartitionSpec as P

gelu_coef = 0.7978845608028654
cubic_coef = 0.044715


def gelu_slope(values):
    inner = gelu_coef * (values + cubic_coef * values * values * values)
    tanh_part = jnp.tanh(inner)
    return 0.5 * (1.0 + tanh_part) + 0.5 * values * (1.0 - tanh_part * tanh_part) * gelu_coef * (
        1.0 + 3.0 * cubic_coef * values * values
    )


def shards(tokens, router, out_grad, slot_outputs, preact, w_in, w_out):
    n_exp = lax.axis_size("expert")
    n_hid = lax.axis_size("hidden")
    own_images = tokens.shape[0]
    feat_dim = tokens.shape[2]
    slot_count = router.shape[1]
    exp_dev = w_in.shape[0]
    experts_all = exp_dev * n_exp
    per_expert = slot_count // experts_all
    all_images = own_images * n_exp * n_hid
    logits = jnp.einsum("bmd,dn->bmn", tokens, router, preferred_element_type=jnp.float32)
    dispatch = jax.nn.softmax(logits, axis=1)
    combine = jax.nn.softmax(logits, axis=2)
    dispatch_b = dispatch.astype(jnp.bfloat16)
    combine_b = combine.astype(jnp.bfloat16)
    grad_combine = jnp.einsum(
        "bmd,bnd->bmn", out_grad, slot_outputs, preferred_element_type=jnp.float32
    )
    slot_grad = jnp.einsum(
        "bmn,bmd->bnd", combine_b, out_grad, preferred_element_type=jnp.float32
    ).astype(jnp.bfloat16)
    devs = n_exp * n_hid
    rows = exp_dev * own_images * per_expert
    both = ("expert", "hidden")
    outbound = slot_grad.reshape(own_images, n_exp, exp_dev, per_expert, feat_dim)
    outbound = outbound.transpose(1, 2, 0, 3, 4).reshape(n_exp, 1, rows, feat_dim)
    outbound = jnp.broadcast_to(outbound, (n_exp, n_hid, rows, feat_dim))
    outbound = outbound.reshape(devs, rows, feat_dim)
    arrived = lax.all_to_all(outbound, both, split_axis=0, concat_axis=0, tiled=True)
    arrived = arrived.reshape(devs, exp_dev, own_images * per_expert, feat_dim)
    grads = arrived.transpose(1, 0, 2, 3).reshape(exp_dev, -1, feat_dim)
    grad_act = jnp.einsum("erd,ehd->erh", grads, w_out, preferred_element_type=jnp.float32)
    grad_pre = (grad_act * gelu_slope(preact.astype(jnp.float32))).astype(jnp.bfloat16)
    partial_in = jnp.einsum("erh,edh->erd", grad_pre, w_in, preferred_element_type=jnp.float32)
    partial_in = partial_in.astype(jnp.bfloat16).reshape(exp_dev, devs, -1, feat_dim)
    partial_in = partial_in.transpose(1, 0, 2, 3).reshape(devs, rows, feat_dim)
    returned = lax.all_to_all(partial_in, both, split_axis=0, concat_axis=0, tiled=True)
    returned = returned.reshape(n_exp, n_hid, rows, feat_dim).astype(jnp.float32)
    summed = jnp.sum(returned, axis=1).astype(jnp.bfloat16)
    summed = summed.reshape(n_exp, exp_dev, own_images, per_expert, feat_dim)
    slot_in_grad = summed.transpose(2, 0, 1, 3, 4).reshape(own_images, slot_count, feat_dim)
    grad_dispatch = jnp.einsum(
        "bmd,bnd->bmn", tokens, slot_in_grad, preferred_element_type=jnp.float32
    )
    part_disp = dispatch * (
        grad_dispatch - jnp.sum(dispatch * grad_dispatch, axis=1, keepdims=True)
    )
    part_comb = combine * (grad_combine - jnp.sum(combine * grad_combine, axis=2, keepdims=True))
    grad_logits = (part_disp + part_comb).astype(jnp.bfloat16)
    through_slots = jnp.einsum(
        "bmn,bnd->bmd", dispatch_b, slot_in_grad, preferred_element_type=jnp.float32
    )
    through_router = jnp.einsum(
        "bmn,dn->bmd", grad_logits, router, preferred_element_type=jnp.float32
    )
    grad_tokens = (through_slots + through_router).astype(jnp.bfloat16)
    router_term = jnp.einsum(
        "bmd,bmn->dn", tokens, grad_logits, preferred_element_type=jnp.float32
    ) * (1.0 / all_images)
    pieces = router_term.astype(jnp.bfloat16).reshape(devs, feat_dim // devs, slot_count)
    pieces = lax.all_to_all(pieces, both, split_axis=0, concat_axis=0, tiled=True)
    grad_router = jnp.sum(pieces.astype(jnp.float32), axis=0)
    return (grad_tokens, grad_router)


def solution(mesh):
    in_specs = (
        P(("expert", "hidden"), None, None),
        P(),
        P(("expert", "hidden"), None, None),
        P(("expert", "hidden"), None, None),
        P("expert", None, "hidden"),
        P("expert", None, "hidden"),
        P("expert", "hidden", None),
    )
    out_specs = (P(("expert", "hidden"), None, None), P(("expert", "hidden"), None))
    return jax.shard_map(shards, mesh=mesh, in_specs=in_specs, out_specs=out_specs, check_vma=False)
```

```python
import functools

import jax
import jax.numpy as jnp
from jax import lax
from jax.experimental import pallas as pl
from jax.experimental.pallas import tpu as pltpu
from jax.sharding import PartitionSpec as P

gelu_coef = 0.7978845608028654
cubic_coef = 0.044715
bf16 = jnp.bfloat16
f32 = jnp.float32
block = 256
vmem_bytes = 40 * 1024 * 1024
in_hbm = pl.BlockSpec(memory_space=pl.ANY)
in_vmem = pl.BlockSpec(memory_space=pltpu.VMEM)


def gelu_slope(values):
    inner = gelu_coef * (values + cubic_coef * values * values * values)
    tanh_part = jnp.tanh(inner)
    return 0.5 * (1.0 + tanh_part) + 0.5 * values * (1.0 - tanh_part * tanh_part) * gelu_coef * (
        1.0 + 3.0 * cubic_coef * values * values
    )


def mm(a, b, over_a=1, over_b=0):
    return lax.dot_general(a, b, (((over_a,), (over_b,)), ((), ())), preferred_element_type=f32)


def softmax(values, axis):
    grown = jnp.exp(values - jnp.max(values, axis=axis, keepdims=True))
    return grown / jnp.sum(grown, axis=axis, keepdims=True)


def one_hot(rows, cols, source):
    r = lax.broadcasted_iota(jnp.int32, (rows, cols), 0)
    c = lax.broadcasted_iota(jnp.int32, (rows, cols), 1)
    return jnp.where(source(r) == c, 1.0, 0.0).astype(bf16)


def slots_kernel(
    tokens_hbm, router_hbm, out_grad_hbm, logits_hbm, send_hbm, tokens, router, out_grad, logits_kept, slot_grad, send,
    sems, send_sems, *, images, rows, n_hid, exp_dev, per
):
    loads = [pltpu.make_async_copy(router_hbm, router, sems.at[2 * images])]
    loads += [pltpu.make_async_copy(tokens_hbm.at[i], tokens.at[i], sems.at[i]) for i in range(images)]
    loads += [pltpu.make_async_copy(out_grad_hbm.at[i], out_grad.at[i], sems.at[images + i]) for i in range(images)]
    for load in loads:
        load.start()
    for load in loads[: images + 1]:
        load.wait()
    combine = []
    for i in range(images):
        logits = mm(tokens[i], router[...])
        logits_kept[i] = logits
        combine.append(softmax(logits, 1).astype(bf16))
    for load in loads[images + 1 :]:
        load.wait()
    for i in range(images):
        slot_grad[i] = mm(combine[i], out_grad[i], 0, 0).astype(bf16)
    own = exp_dev * per
    take = block // (n_hid * rows) * own

    def source(r):
        dest, at = r // (n_hid * rows), r % rows
        exp, img, s = at // (images * per), (at // per) % images, at % per
        return img * take + dest * own + exp * per + s

    pick = one_hot(block, images * take, source)
    copies = []
    for k in range(send.shape[0] // block):
        parts = [slot_grad[m, k * take : (k + 1) * take, :] for m in range(images)]
        at = pl.ds(k * block, block)
        send[at, :] = mm(pick, jnp.concatenate(parts, axis=0)).astype(bf16)
        copies.append(pltpu.make_async_copy(send.at[at], send_hbm.at[at], send_sems.at[k]))
        copies[-1].start()
    copies.append(pltpu.make_async_copy(logits_kept, logits_hbm, send_sems.at[len(copies)]))
    copies[-1].start()
    for copy in copies:
        copy.wait()


def experts_kernel(
    recv_ref, slope_hbm, w_in_hbm, w_out_hbm, send_hbm, slope, w_in, w_out, grads, grad_pre, back, send, sems, send_sems,
    *, exp_dev, rows
):
    hid = slope.shape[2]
    first = [pl.ds(0, hid // 4), pl.ds(hid // 4, hid // 4), pl.ds(hid // 2, hid // 2)]
    units = [first] + [[pl.ds(0, hid)]] * (exp_dev - 1)
    loads = []
    for e in range(exp_dev):
        for at in units[e]:
            loads.append((w_out_hbm.at[e, at], w_out.at[e, at]))
            loads.append((slope_hbm.at[e, :, at], slope.at[e, :, at]))
        loads.append((w_in_hbm.at[e], w_in.at[e]))
    loads = [pltpu.make_async_copy(a, b, sems.at[n]) for n, (a, b) in enumerate(loads)]
    for load in loads:
        load.start()
    own = rows // exp_dev
    take = block // exp_dev
    blocks = recv_ref.shape[0] // block
    pick = one_hot(block, block, lambda r: (r % take // own) * rows + r // take * own + r % own)
    for k in range(blocks):
        picked = mm(pick, recv_ref[k * block : (k + 1) * block, :]).astype(bf16)
        for e in range(exp_dev):
            grads[e, k * take : (k + 1) * take, :] = picked[e * take : (e + 1) * take, :]
    n = 0
    for e in range(exp_dev):
        for at in units[e]:
            loads[n].wait()
            loads[n + 1].wait()
            grad_act = mm(grads[e], w_out[e, at, :], 1, 1)
            grad_pre[:, at] = (grad_act * slope[e, :, at].astype(f32)).astype(bf16)
            n += 2
        loads[n].wait()
        back[e] = mm(grad_pre[...], w_in[e], 1, 1).astype(bf16)
        n += 1
    pick = one_hot(block, block, lambda r: (r % rows // own) * take + r // rows * own + r % own)
    copies = []
    for k in range(blocks):
        parts = [back[e, k * take : (k + 1) * take, :] for e in range(exp_dev)]
        at = pl.ds(k * block, block)
        send[at, :] = mm(pick, jnp.concatenate(parts, axis=0)).astype(bf16)
        copies.append(pltpu.make_async_copy(send.at[at], send_hbm.at[at], send_sems.at[k]))
        copies[-1].start()
    for copy in copies:
        copy.wait()


def combine_kernel(
    logits_ref, tokens_ref, out_grad_ref, slot_outputs_ref, turned_ref, dispatch_ref, weights_ref, part_ref
):
    images, toks = logits_ref.shape[:2]
    for i in range(images):
        dispatch = softmax(logits_ref[i], 0)
        dispatch_ref[i] = dispatch
        weights_ref[i] = dispatch.astype(bf16)
        combine = softmax(logits_ref[i], 1)
        grad = mm(out_grad_ref[i], slot_outputs_ref[i], 1, 1)
        part_ref[i] = combine * (grad - jnp.sum(combine * grad, axis=1, keepdims=True))
        turned_ref[:, i * toks : (i + 1) * toks] = jnp.transpose(tokens_ref[i])


def logits_kernel(
    recv_ref, tokens_hbm, turned_hbm, dispatch_hbm, part_hbm, slot_hbm, grad_hbm, router_hbm,
    tokens, turned, dispatch, part, slot_in, grad_logits, router_term, sems, *, images, rows, n_hid, exp_dev, per
):
    loads = [(tokens_hbm, tokens), (dispatch_hbm, dispatch), (part_hbm, part), (turned_hbm, turned)]
    loads = [pltpu.make_async_copy(a, b, sems.at[n]) for n, (a, b) in enumerate(loads)]
    for load in loads:
        load.start()
    feat = recv_ref.shape[1]
    own = exp_dev * per
    take = block // images

    def source(r):
        img, dest, exp, s = r // take, r % take // own, r % own // per, r % per
        return dest * rows + exp * images * per + img * per + s

    pick = one_hot(block, block, source)
    for k in range(recv_ref.shape[0] // (n_hid * block)):
        halves = recv_ref[k * n_hid * block : (k + 1) * n_hid * block, :].astype(f32)
        halves = halves.reshape(block // rows, n_hid, rows, feat)
        summed = halves[:, 0]
        for h in range(1, n_hid):
            summed = summed + halves[:, h]
        picked = mm(pick, summed.reshape(block, feat).astype(bf16)).astype(bf16)
        for i in range(images):
            slot_in[i, k * take : (k + 1) * take, :] = picked[i * take : (i + 1) * take, :]
    copies = [pltpu.make_async_copy(slot_in, slot_hbm, sems.at[len(loads)])]
    copies[-1].start()
    for load in loads[:3]:
        load.wait()
    for i in range(images):
        weights = dispatch[i]
        grad_dispatch = mm(tokens[i], slot_in[i], 1, 1)
        weighed = jnp.sum(weights * grad_dispatch, axis=0, keepdims=True)
        grad_logits[i] = (weights * (grad_dispatch - weighed) + part[i]).astype(bf16)
    copies.append(pltpu.make_async_copy(grad_logits, grad_hbm, sems.at[len(loads) + 1]))
    copies[-1].start()
    loads[3].wait()
    half = feat // 2
    for k in range(2):
        at = pl.ds(k * half, half)
        grads = jnp.concatenate([grad_logits[i] for i in range(images)], axis=0)
        router_term[at, :] = mm(turned[at, :], grads).astype(bf16)
        copies.append(pltpu.make_async_copy(router_term.at[at], router_hbm.at[at], sems.at[len(loads) + 2 + k]))
        copies[-1].start()
    for copy in copies:
        copy.wait()


def shards(tokens, router, out_grad, slot_outputs, preact, w_in, w_out):
    n_exp = lax.axis_size("expert")
    n_hid = lax.axis_size("hidden")
    both = ("expert", "hidden")
    devs = n_exp * n_hid
    images, toks, feat = tokens.shape
    slots = router.shape[1]
    exp_dev, exp_rows, hid = preact.shape
    per = slots // (exp_dev * n_exp)
    rows = images * exp_dev * per
    all_rows = devs * rows
    sizes = dict(images=images, rows=rows, n_hid=n_hid, exp_dev=exp_dev, per=per)
    dma = pltpu.SemaphoreType.DMA

    def exchange(x):
        split = x.reshape(devs, -1, x.shape[1])
        return lax.all_to_all(split, both, split_axis=0, concat_axis=0, tiled=True)

    def call(kernel, ins, outs, outs_in, scratch, flops, moved, name):
        kept = pl.pallas_call(
            kernel,
            in_specs=ins,
            out_specs=[outs_in] * len(outs),
            out_shape=[pltpu.HBM(*o) for o in outs],
            scratch_shapes=scratch,
            compiler_params=pltpu.CompilerParams(vmem_limit_bytes=vmem_bytes),
            cost_estimate=pl.CostEstimate(flops=flops, transcendentals=0, bytes_accessed=moved),
            name=name,
        )
        return lambda *xs: kept(*[hold(x) if i is in_hbm else x for i, x in zip(ins, xs)])

    def hold(x):
        return pltpu.with_memory_space_constraint(x, pltpu.HBM)

    per_image = 2 * images * toks * slots * feat
    logit_shape = (images, toks, slots)
    slot_shape = (images, slots, feat)
    logits, send = call(
        functools.partial(slots_kernel, **sizes),
        [in_hbm] * 3,
        [(logit_shape, f32), ((all_rows, feat), bf16)],
        in_hbm,
        [
            pltpu.VMEM(tokens.shape, bf16),
            pltpu.VMEM(router.shape, bf16),
            pltpu.VMEM(out_grad.shape, bf16),
            pltpu.VMEM(logit_shape, f32),
            pltpu.VMEM(slot_shape, bf16),
            pltpu.VMEM((all_rows, feat), bf16),
            dma((2 * images + 1,)),
            dma((1 + all_rows // block,)),
        ],
        2 * per_image,
        6 << 20,
        "slots",
    )(tokens, router, out_grad)

    arrived = exchange(send)
    preact, _ = lax.optimization_barrier((preact, send))
    slope = gelu_slope(preact.astype(f32)).astype(bf16)

    partial_in = call(
        functools.partial(experts_kernel, exp_dev=exp_dev, rows=rows),
        [in_vmem] + [in_hbm] * 3,
        [((all_rows, feat), bf16)],
        in_hbm,
        [
            pltpu.VMEM(preact.shape, bf16),
            pltpu.VMEM(w_in.shape, bf16),
            pltpu.VMEM(w_out.shape, bf16),
            pltpu.VMEM((exp_dev, exp_rows, feat), bf16),
            pltpu.VMEM((exp_rows, hid), bf16),
            pltpu.VMEM((exp_dev, exp_rows, feat), bf16),
            pltpu.VMEM((all_rows, feat), bf16),
            dma((3 * exp_dev + 4,)),
            dma((all_rows // block,)),
        ],
        4 * exp_dev * exp_rows * feat * hid,
        24 << 20,
        "experts",
    )(arrived.reshape(all_rows, feat), slope, w_in, w_out)[0]

    returned = exchange(partial_in)
    logits, _ = lax.optimization_barrier((logits, partial_in))
    turned, dispatch, weights, part_comb = call(
        combine_kernel,
        [in_vmem] * 4,
        [((feat, images * toks), bf16), (logit_shape, f32), (logit_shape, bf16), (logit_shape, f32)],
        in_vmem,
        [],
        per_image,
        8 << 20,
        "combine",
    )(logits, tokens, out_grad, slot_outputs)

    slot_in_grad, grad_logits, router_term = call(
        functools.partial(logits_kernel, **sizes),
        [in_vmem] + [in_hbm] * 4,
        [(slot_shape, bf16), (logit_shape, bf16), (router.shape, bf16)],
        in_hbm,
        [
            pltpu.VMEM(tokens.shape, bf16),
            pltpu.VMEM((feat, images * toks), bf16),
            pltpu.VMEM(logit_shape, f32),
            pltpu.VMEM(logit_shape, f32),
            pltpu.VMEM(slot_shape, bf16),
            pltpu.VMEM(logit_shape, bf16),
            pltpu.VMEM(router.shape, bf16),
            dma((8,)),
        ],
        3 * per_image,
        6 << 20,
        "logit_grads",
    )(returned.reshape(all_rows, feat), tokens, turned, dispatch, part_comb)

    pieces = exchange(router_term)
    through_slots = jnp.einsum("bmn,bnd->bmd", weights, slot_in_grad, preferred_element_type=f32)
    through_router = jnp.einsum("bmn,dn->bmd", grad_logits, router, preferred_element_type=f32)
    grad_tokens = (through_slots + through_router).astype(bf16)
    grad_router = jnp.sum(pieces.astype(f32) * (1.0 / (images * devs)), axis=0)
    return (grad_tokens, grad_router)


def solution(mesh):
    in_specs = (
        P(("expert", "hidden"), None, None),
        P(),
        P(("expert", "hidden"), None, None),
        P(("expert", "hidden"), None, None),
        P("expert", None, "hidden"),
        P("expert", None, "hidden"),
        P("expert", "hidden", None),
    )
    out_specs = (P(("expert", "hidden"), None, None), P(("expert", "hidden"), None))
    return jax.shard_map(shards, mesh=mesh, in_specs=in_specs, out_specs=out_specs, check_vma=False)
```

```python
import functools

import jax
import jax.numpy as jnp
from jax import lax
from jax.experimental import pallas as pl
from jax.experimental.pallas import tpu as pltpu
from jax.sharding import PartitionSpec as P

gelu_coef = 0.7978845608028654
cubic_coef = 0.044715
bf16 = jnp.bfloat16
f32 = jnp.float32
block = 256
in_hbm = pl.BlockSpec(memory_space=pl.ANY)
in_vmem = pl.BlockSpec(memory_space=pltpu.VMEM)


def gelu_slope(values):
    inner = gelu_coef * (values + cubic_coef * values * values * values)
    tanh_part = jnp.tanh(inner)
    return 0.5 * (1.0 + tanh_part) + 0.5 * values * (1.0 - tanh_part * tanh_part) * gelu_coef * (
        1.0 + 3.0 * cubic_coef * values * values
    )


def mm(a, b, over_a=1, over_b=0):
    return lax.dot_general(a, b, (((over_a,), (over_b,)), ((), ())), preferred_element_type=f32)


def softmax(values, axis):
    grown = jnp.exp(values - jnp.max(values, axis=axis, keepdims=True))
    return grown / jnp.sum(grown, axis=axis, keepdims=True)


def one_hot(rows, cols, source):
    r = lax.broadcasted_iota(jnp.int32, (rows, cols), 0)
    c = lax.broadcasted_iota(jnp.int32, (rows, cols), 1)
    return jnp.where(source(r) == c, 1.0, 0.0).astype(bf16)


def slots_kernel(
    tokens_hbm, router_hbm, out_grad_hbm, logits_hbm, send_ref, tokens, router, out_grad, logits_kept, slot_grad,
    sems, send_sem, *, images, rows, n_hid, exp_dev, per
):
    loads = [pltpu.make_async_copy(router_hbm, router, sems.at[2 * images])]
    loads += [pltpu.make_async_copy(tokens_hbm.at[i], tokens.at[i], sems.at[i]) for i in range(images)]
    loads += [pltpu.make_async_copy(out_grad_hbm.at[i], out_grad.at[i], sems.at[images + i]) for i in range(images)]
    for load in loads:
        load.start()
    for load in loads[: images + 1]:
        load.wait()
    combine = []
    for i in range(images):
        logits = mm(tokens[i], router[...])
        logits_kept[i] = logits
        combine.append(softmax(logits, 1).astype(bf16))
    for load in loads[images + 1 :]:
        load.wait()
    for i in range(images):
        slot_grad[i] = mm(combine[i], out_grad[i], 0, 0).astype(bf16)
    own = exp_dev * per
    take = block // (n_hid * rows) * own

    def source(r):
        dest, at = r // (n_hid * rows), r % rows
        exp, img, s = at // (images * per), (at // per) % images, at % per
        return img * take + dest * own + exp * per + s

    copy = pltpu.make_async_copy(logits_kept, logits_hbm, send_sem)
    copy.start()
    pick = one_hot(block, images * take, source)
    for k in range(send_ref.shape[0] // block):
        parts = [slot_grad[m, k * take : (k + 1) * take, :] for m in range(images)]
        send_ref[k * block : (k + 1) * block, :] = mm(pick, jnp.concatenate(parts, axis=0)).astype(bf16)
    copy.wait()


def experts_kernel(recv_ref, preact_ref, w_in_ref, w_out_ref, send_hbm, grads, grad_pre, back, send, send_sems, *, exp_dev, rows):
    own = rows // exp_dev
    take = block // exp_dev
    blocks = recv_ref.shape[0] // block
    pick = one_hot(block, block, lambda r: (r % take // own) * rows + r // take * own + r % own)
    for k in range(blocks):
        picked = mm(pick, recv_ref[k * block : (k + 1) * block, :]).astype(bf16)
        for e in range(exp_dev):
            grads[e, k * take : (k + 1) * take, :] = picked[e * take : (e + 1) * take, :]
    for e in range(exp_dev):
        for k in range(w_out_ref.shape[1] // block):
            at = slice(k * block, (k + 1) * block)
            grad_act = mm(grads[e], w_out_ref[e, at, :], 1, 1)
            grad_pre[:, at] = (grad_act * gelu_slope(preact_ref[e, :, at].astype(f32))).astype(bf16)
        back[e] = mm(grad_pre[...], w_in_ref[e], 1, 1).astype(bf16)
    pick = one_hot(block, block, lambda r: (r % rows // own) * take + r // rows * own + r % own)
    copies = []
    for k in range(blocks):
        parts = [back[e, k * take : (k + 1) * take, :] for e in range(exp_dev)]
        at = pl.ds(k * block, block)
        send[at, :] = mm(pick, jnp.concatenate(parts, axis=0)).astype(bf16)
        copies.append(pltpu.make_async_copy(send.at[at], send_hbm.at[at], send_sems.at[k]))
        copies[-1].start()
    for copy in copies:
        copy.wait()


def combine_kernel(
    logits_ref, tokens_ref, out_grad_ref, slot_outputs_ref, turned_ref, dispatch_ref, weights_ref, part_ref
):
    images, toks = logits_ref.shape[:2]
    for i in range(images):
        dispatch = softmax(logits_ref[i], 0)
        dispatch_ref[i] = dispatch
        weights_ref[i] = dispatch.astype(bf16)
        combine = softmax(logits_ref[i], 1)
        grad = mm(out_grad_ref[i], slot_outputs_ref[i], 1, 1)
        part_ref[i] = combine * (grad - jnp.sum(combine * grad, axis=1, keepdims=True))
        turned_ref[:, i * toks : (i + 1) * toks] = jnp.transpose(tokens_ref[i])


def logits_kernel(
    recv_ref, tokens_hbm, turned_hbm, dispatch_hbm, part_hbm, slot_hbm, grad_hbm, router_hbm,
    tokens, turned, dispatch, part, slot_in, grad_logits, router_term, sems, *, images, rows, n_hid, exp_dev, per
):
    loads = [(tokens_hbm, tokens), (dispatch_hbm, dispatch), (part_hbm, part), (turned_hbm, turned)]
    loads = [pltpu.make_async_copy(a, b, sems.at[n]) for n, (a, b) in enumerate(loads)]
    for load in loads:
        load.start()
    feat = recv_ref.shape[1]
    own = exp_dev * per
    take = block // images

    def source(r):
        img, dest, exp, s = r // take, r % take // own, r % own // per, r % per
        return dest * rows + exp * images * per + img * per + s

    pick = one_hot(block, block, source)
    for k in range(recv_ref.shape[0] // (n_hid * block)):
        halves = recv_ref[k * n_hid * block : (k + 1) * n_hid * block, :].astype(f32)
        halves = halves.reshape(block // rows, n_hid, rows, feat)
        summed = halves[:, 0]
        for h in range(1, n_hid):
            summed = summed + halves[:, h]
        picked = mm(pick, summed.reshape(block, feat).astype(bf16)).astype(bf16)
        for i in range(images):
            slot_in[i, k * take : (k + 1) * take, :] = picked[i * take : (i + 1) * take, :]
    copies = [pltpu.make_async_copy(slot_in, slot_hbm, sems.at[len(loads)])]
    copies[-1].start()
    for load in loads[:3]:
        load.wait()
    for i in range(images):
        weights = dispatch[i]
        grad_dispatch = mm(tokens[i], slot_in[i], 1, 1)
        weighed = jnp.sum(weights * grad_dispatch, axis=0, keepdims=True)
        grad_logits[i] = (weights * (grad_dispatch - weighed) + part[i]).astype(bf16)
    copies.append(pltpu.make_async_copy(grad_logits, grad_hbm, sems.at[len(loads) + 1]))
    copies[-1].start()
    loads[3].wait()
    half = feat // 2
    for k in range(2):
        at = pl.ds(k * half, half)
        grads = jnp.concatenate([grad_logits[i] for i in range(images)], axis=0)
        router_term[at, :] = mm(turned[at, :], grads).astype(bf16)
        copies.append(pltpu.make_async_copy(router_term.at[at], router_hbm.at[at], sems.at[len(loads) + 2 + k]))
        copies[-1].start()
    for copy in copies:
        copy.wait()


def shards(tokens, router, out_grad, slot_outputs, preact, w_in, w_out):
    n_exp = lax.axis_size("expert")
    n_hid = lax.axis_size("hidden")
    both = ("expert", "hidden")
    devs = n_exp * n_hid
    images, toks, feat = tokens.shape
    slots = router.shape[1]
    exp_dev, exp_rows, hid = preact.shape
    per = slots // (exp_dev * n_exp)
    rows = images * exp_dev * per
    all_rows = devs * rows
    sizes = dict(images=images, rows=rows, n_hid=n_hid, exp_dev=exp_dev, per=per)
    dma = pltpu.SemaphoreType.DMA

    def exchange(x):
        split = x.reshape(devs, -1, x.shape[1])
        return lax.all_to_all(split, both, split_axis=0, concat_axis=0, tiled=True)

    def call(kernel, ins, outs, outs_in, scratch, flops, moved, name, mebibytes=40, near=()):
        kept = pl.pallas_call(
            kernel,
            in_specs=ins,
            out_specs=[in_vmem if n in near else outs_in for n in range(len(outs))],
            out_shape=[(pltpu.VMEM if n in near else pltpu.HBM)(*o) for n, o in enumerate(outs)],
            scratch_shapes=scratch,
            compiler_params=pltpu.CompilerParams(vmem_limit_bytes=mebibytes << 20),
            cost_estimate=pl.CostEstimate(flops=flops, transcendentals=0, bytes_accessed=moved),
            name=name,
        )
        return lambda *xs: kept(*[hold(x) if i is in_hbm else x for i, x in zip(ins, xs)])

    def hold(x):
        return pltpu.with_memory_space_constraint(x, pltpu.HBM)

    per_image = 2 * images * toks * slots * feat
    logit_shape = (images, toks, slots)
    slot_shape = (images, slots, feat)
    logits, send = call(
        functools.partial(slots_kernel, **sizes),
        [in_hbm] * 3,
        [(logit_shape, f32), ((all_rows, feat), bf16)],
        in_hbm,
        [
            pltpu.VMEM(tokens.shape, bf16),
            pltpu.VMEM(router.shape, bf16),
            pltpu.VMEM(out_grad.shape, bf16),
            pltpu.VMEM(logit_shape, f32),
            pltpu.VMEM(slot_shape, bf16),
            dma((2 * images + 1,)),
            dma,
        ],
        40 * per_image,
        6 << 20,
        "slots",
        12,
        (1,),
    )(tokens, router, out_grad)

    arrived = exchange(send)
    preact, w_in, w_out = [pltpu.with_memory_space_constraint(x, pltpu.VMEM) for x in (preact, w_in, w_out)]
    partial_in = call(
        functools.partial(experts_kernel, exp_dev=exp_dev, rows=rows),
        [in_vmem] * 4,
        [((all_rows, feat), bf16)],
        in_hbm,
        [
            pltpu.VMEM((exp_dev, exp_rows, feat), bf16),
            pltpu.VMEM((exp_rows, hid), bf16),
            pltpu.VMEM((exp_dev, exp_rows, feat), bf16),
            pltpu.VMEM((all_rows, feat), bf16),
            dma((all_rows // block,)),
        ],
        4 * exp_dev * exp_rows * feat * hid,
        4 << 20,
        "experts",
        24,
    )(arrived.reshape(all_rows, feat), preact, w_in, w_out)[0]

    returned = exchange(partial_in)
    logits, _ = lax.optimization_barrier((logits, partial_in))
    turned, dispatch, weights, part_comb = call(
        combine_kernel,
        [in_vmem] * 4,
        [((feat, images * toks), bf16), (logit_shape, f32), (logit_shape, bf16), (logit_shape, f32)],
        in_vmem,
        [],
        per_image,
        8 << 20,
        "combine",
    )(logits, tokens, out_grad, slot_outputs)

    slot_in_grad, grad_logits, router_term = call(
        functools.partial(logits_kernel, **sizes),
        [in_vmem] + [in_hbm] * 4,
        [(slot_shape, bf16), (logit_shape, bf16), (router.shape, bf16)],
        in_hbm,
        [
            pltpu.VMEM(tokens.shape, bf16),
            pltpu.VMEM((feat, images * toks), bf16),
            pltpu.VMEM(logit_shape, f32),
            pltpu.VMEM(logit_shape, f32),
            pltpu.VMEM(slot_shape, bf16),
            pltpu.VMEM(logit_shape, bf16),
            pltpu.VMEM(router.shape, bf16),
            dma((8,)),
        ],
        3 * per_image,
        6 << 20,
        "logit_grads",
    )(returned.reshape(all_rows, feat), tokens, turned, dispatch, part_comb)

    pieces = exchange(router_term)
    through_slots = jnp.einsum("bmn,bnd->bmd", weights, slot_in_grad, preferred_element_type=f32)
    through_router = jnp.einsum("bmn,dn->bmd", grad_logits, router, preferred_element_type=f32)
    grad_tokens = (through_slots + through_router).astype(bf16)
    grad_router = jnp.sum(pieces.astype(f32) * (1.0 / (images * devs)), axis=0)
    return (grad_tokens, grad_router)


def solution(mesh):
    in_specs = (
        P(("expert", "hidden"), None, None),
        P(),
        P(("expert", "hidden"), None, None),
        P(("expert", "hidden"), None, None),
        P("expert", None, "hidden"),
        P("expert", None, "hidden"),
        P("expert", "hidden", None),
    )
    out_specs = (P(("expert", "hidden"), None, None), P(("expert", "hidden"), None))
    return jax.shard_map(shards, mesh=mesh, in_specs=in_specs, out_specs=out_specs, check_vma=False)
```

```python
import functools

import jax
import jax.numpy as jnp
from jax import lax
from jax.experimental import pallas as pl
from jax.experimental.pallas import tpu as pltpu
from jax.sharding import PartitionSpec as P

gelu_coef = 0.7978845608028654
cubic_coef = 0.044715
bf16 = jnp.bfloat16
f32 = jnp.float32
block = 256
in_hbm = pl.BlockSpec(memory_space=pl.ANY)
in_vmem = pl.BlockSpec(memory_space=pltpu.VMEM)


def gelu_slope(values):
    inner = gelu_coef * (values + cubic_coef * values * values * values)
    tanh_part = jnp.tanh(inner)
    return 0.5 * (1.0 + tanh_part) + 0.5 * values * (1.0 - tanh_part * tanh_part) * gelu_coef * (
        1.0 + 3.0 * cubic_coef * values * values
    )


def mm(a, b, over_a=1, over_b=0):
    return lax.dot_general(a, b, (((over_a,), (over_b,)), ((), ())), preferred_element_type=f32)


def softmax(values, axis):
    grown = jnp.exp(values - jnp.max(values, axis=axis, keepdims=True))
    return grown / jnp.sum(grown, axis=axis, keepdims=True)


def one_hot(rows, cols, source):
    r = lax.broadcasted_iota(jnp.int32, (rows, cols), 0)
    c = lax.broadcasted_iota(jnp.int32, (rows, cols), 1)
    return jnp.where(source(r) == c, 1.0, 0.0).astype(bf16)


def slots_kernel(
    tokens_hbm, router_hbm, out_grad_hbm, logits_hbm, send_ref, tokens, router, out_grad, logits_kept, slot_grad,
    sems, send_sem, *, images, rows, n_hid, exp_dev, per
):
    loads = [pltpu.make_async_copy(router_hbm, router, sems.at[2 * images])]
    loads += [pltpu.make_async_copy(tokens_hbm.at[i], tokens.at[i], sems.at[i]) for i in range(images)]
    loads += [pltpu.make_async_copy(out_grad_hbm.at[i], out_grad.at[i], sems.at[images + i]) for i in range(images)]
    for load in loads:
        load.start()
    for load in loads[: images + 1]:
        load.wait()
    combine = []
    for i in range(images):
        logits = mm(tokens[i], router[...])
        logits_kept[i] = logits
        combine.append(softmax(logits, 1).astype(bf16))
    for load in loads[images + 1 :]:
        load.wait()
    for i in range(images):
        slot_grad[i] = mm(combine[i], out_grad[i], 0, 0).astype(bf16)
    own = exp_dev * per
    take = block // (n_hid * rows) * own

    def source(r):
        dest, at = r // (n_hid * rows), r % rows
        exp, img, s = at // (images * per), (at // per) % images, at % per
        return img * take + dest * own + exp * per + s

    copy = pltpu.make_async_copy(logits_kept, logits_hbm, send_sem)
    copy.start()
    pick = one_hot(block, images * take, source)
    for k in range(send_ref.shape[0] // block):
        parts = [slot_grad[m, k * take : (k + 1) * take, :] for m in range(images)]
        send_ref[k * block : (k + 1) * block, :] = mm(pick, jnp.concatenate(parts, axis=0)).astype(bf16)
    copy.wait()


def experts_kernel(recv_ref, preact_ref, w_in_ref, w_out_ref, send_hbm, grads, grad_pre, back, send, send_sems, *, exp_dev, rows):
    own = rows // exp_dev
    take = block // exp_dev
    blocks = recv_ref.shape[0] // block
    pick = one_hot(block, block, lambda r: (r % take // own) * rows + r // take * own + r % own)
    for k in range(blocks):
        picked = mm(pick, recv_ref[k * block : (k + 1) * block, :]).astype(bf16)
        for e in range(exp_dev):
            grads[e, k * take : (k + 1) * take, :] = picked[e * take : (e + 1) * take, :]
    units, feats = w_out_ref.shape[1] // block, w_out_ref.shape[2] // block
    for e in range(exp_dev + 1):
        for k in range(units):
            at = slice(k * block, (k + 1) * block)
            if e < exp_dev:
                grad_act = mm(grads[e], w_out_ref[e, at, :], 1, 1)
                grad_pre[e, :, at] = (grad_act * gelu_slope(preact_ref[e, :, at].astype(f32))).astype(bf16)
                if 0 < e and k < feats:
                    back[e - 1, :, at] = mm(grad_pre[e - 1], w_in_ref[e - 1, at, :], 1, 1).astype(bf16)
        if e == exp_dev:
            back[e - 1] = mm(grad_pre[e - 1], w_in_ref[e - 1], 1, 1).astype(bf16)
    pick = one_hot(block, block, lambda r: (r % rows // own) * take + r // rows * own + r % own)
    copies = []
    for k in range(blocks):
        parts = [back[e, k * take : (k + 1) * take, :] for e in range(exp_dev)]
        at = pl.ds(k * block, block)
        send[at, :] = mm(pick, jnp.concatenate(parts, axis=0)).astype(bf16)
        copies.append(pltpu.make_async_copy(send.at[at], send_hbm.at[at], send_sems.at[k]))
        copies[-1].start()
    for copy in copies:
        copy.wait()


def combine_kernel(
    logits_ref, tokens_ref, out_grad_ref, slot_outputs_ref, turned_ref, dispatch_ref, weights_ref, part_ref
):
    images, toks = logits_ref.shape[:2]
    for i in range(images):
        dispatch = softmax(logits_ref[i], 0)
        dispatch_ref[i] = dispatch
        weights_ref[i] = dispatch.astype(bf16)
        combine = softmax(logits_ref[i], 1)
        grad = mm(out_grad_ref[i], slot_outputs_ref[i], 1, 1)
        part_ref[i] = combine * (grad - jnp.sum(combine * grad, axis=1, keepdims=True))
        turned_ref[:, i * toks : (i + 1) * toks] = jnp.transpose(tokens_ref[i])


def logits_kernel(
    recv_ref, tokens_hbm, turned_hbm, dispatch_hbm, part_hbm, slot_hbm, grad_hbm, router_hbm,
    tokens, turned, dispatch, part, slot_in, grad_logits, router_term, sems, *, images, rows, n_hid, exp_dev, per
):
    loads = [(tokens_hbm, tokens), (dispatch_hbm, dispatch), (part_hbm, part), (turned_hbm, turned)]
    loads = [pltpu.make_async_copy(a, b, sems.at[n]) for n, (a, b) in enumerate(loads)]
    for load in loads:
        load.start()
    feat = recv_ref.shape[1]
    own = exp_dev * per
    take = block // images

    def source(r):
        img, dest, exp, s = r // take, r % take // own, r % own // per, r % per
        return dest * rows + exp * images * per + img * per + s

    pick = one_hot(block, block, source)
    for k in range(recv_ref.shape[0] // (n_hid * block)):
        halves = recv_ref[k * n_hid * block : (k + 1) * n_hid * block, :].astype(f32)
        halves = halves.reshape(block // rows, n_hid, rows, feat)
        summed = halves[:, 0]
        for h in range(1, n_hid):
            summed = summed + halves[:, h]
        picked = mm(pick, summed.reshape(block, feat).astype(bf16)).astype(bf16)
        for i in range(images):
            slot_in[i, k * take : (k + 1) * take, :] = picked[i * take : (i + 1) * take, :]
    copies = [pltpu.make_async_copy(slot_in, slot_hbm, sems.at[len(loads)])]
    copies[-1].start()
    for load in loads[:3]:
        load.wait()
    for i in range(images):
        weights = dispatch[i]
        grad_dispatch = mm(tokens[i], slot_in[i], 1, 1)
        weighed = jnp.sum(weights * grad_dispatch, axis=0, keepdims=True)
        grad_logits[i] = (weights * (grad_dispatch - weighed) + part[i]).astype(bf16)
    copies.append(pltpu.make_async_copy(grad_logits, grad_hbm, sems.at[len(loads) + 1]))
    copies[-1].start()
    loads[3].wait()
    half = feat // 2
    for k in range(2):
        at = pl.ds(k * half, half)
        grads = jnp.concatenate([grad_logits[i] for i in range(images)], axis=0)
        router_term[at, :] = mm(turned[at, :], grads).astype(bf16)
        copies.append(pltpu.make_async_copy(router_term.at[at], router_hbm.at[at], sems.at[len(loads) + 2 + k]))
        copies[-1].start()
    for copy in copies:
        copy.wait()


def shards(tokens, router, out_grad, slot_outputs, preact, w_in, w_out):
    n_exp = lax.axis_size("expert")
    n_hid = lax.axis_size("hidden")
    both = ("expert", "hidden")
    devs = n_exp * n_hid
    images, toks, feat = tokens.shape
    slots = router.shape[1]
    exp_dev, exp_rows, hid = preact.shape
    per = slots // (exp_dev * n_exp)
    rows = images * exp_dev * per
    all_rows = devs * rows
    sizes = dict(images=images, rows=rows, n_hid=n_hid, exp_dev=exp_dev, per=per)
    dma = pltpu.SemaphoreType.DMA

    def exchange(x):
        split = x.reshape(devs, -1, x.shape[1])
        return lax.all_to_all(split, both, split_axis=0, concat_axis=0, tiled=True)

    def call(kernel, ins, outs, outs_in, scratch, flops, moved, name, mebibytes=40, near=()):
        kept = pl.pallas_call(
            kernel,
            in_specs=ins,
            out_specs=[in_vmem if n in near else outs_in for n in range(len(outs))],
            out_shape=[(pltpu.VMEM if n in near else pltpu.HBM)(*o) for n, o in enumerate(outs)],
            scratch_shapes=scratch,
            compiler_params=pltpu.CompilerParams(vmem_limit_bytes=mebibytes << 20),
            cost_estimate=pl.CostEstimate(flops=flops, transcendentals=0, bytes_accessed=moved),
            name=name,
        )
        return lambda *xs: kept(*[hold(x) if i is in_hbm else x for i, x in zip(ins, xs)])

    def hold(x):
        return pltpu.with_memory_space_constraint(x, pltpu.HBM)

    per_image = 2 * images * toks * slots * feat
    logit_shape = (images, toks, slots)
    slot_shape = (images, slots, feat)
    logits, send = call(
        functools.partial(slots_kernel, **sizes),
        [in_hbm] * 3,
        [(logit_shape, f32), ((all_rows, feat), bf16)],
        in_hbm,
        [
            pltpu.VMEM(tokens.shape, bf16),
            pltpu.VMEM(router.shape, bf16),
            pltpu.VMEM(out_grad.shape, bf16),
            pltpu.VMEM(logit_shape, f32),
            pltpu.VMEM(slot_shape, bf16),
            dma((2 * images + 1,)),
            dma,
        ],
        40 * per_image,
        6 << 20,
        "slots",
        12,
        (1,),
    )(tokens, router, out_grad)

    arrived = exchange(send)
    preact, w_in, w_out = [pltpu.with_memory_space_constraint(x, pltpu.VMEM) for x in (preact, w_in, w_out)]
    partial_in = call(
        functools.partial(experts_kernel, exp_dev=exp_dev, rows=rows),
        [in_vmem] * 4,
        [((all_rows, feat), bf16)],
        in_hbm,
        [
            pltpu.VMEM((exp_dev, exp_rows, feat), bf16),
            pltpu.VMEM((exp_dev, exp_rows, hid), bf16),
            pltpu.VMEM((exp_dev, exp_rows, feat), bf16),
            pltpu.VMEM((all_rows, feat), bf16),
            dma((all_rows // block,)),
        ],
        4 * exp_dev * exp_rows * feat * hid,
        4 << 20,
        "experts",
        28,
    )(arrived.reshape(all_rows, feat), preact, w_in, w_out)[0]

    returned = exchange(partial_in)
    logits, _ = lax.optimization_barrier((logits, partial_in))
    turned, dispatch, weights, part_comb = call(
        combine_kernel,
        [in_vmem] * 4,
        [((feat, images * toks), bf16), (logit_shape, f32), (logit_shape, bf16), (logit_shape, f32)],
        in_vmem,
        [],
        per_image,
        8 << 20,
        "combine",
    )(logits, tokens, out_grad, slot_outputs)

    slot_in_grad, grad_logits, router_term = call(
        functools.partial(logits_kernel, **sizes),
        [in_vmem] + [in_hbm] * 4,
        [(slot_shape, bf16), (logit_shape, bf16), (router.shape, bf16)],
        in_hbm,
        [
            pltpu.VMEM(tokens.shape, bf16),
            pltpu.VMEM((feat, images * toks), bf16),
            pltpu.VMEM(logit_shape, f32),
            pltpu.VMEM(logit_shape, f32),
            pltpu.VMEM(slot_shape, bf16),
            pltpu.VMEM(logit_shape, bf16),
            pltpu.VMEM(router.shape, bf16),
            dma((8,)),
        ],
        3 * per_image,
        6 << 20,
        "logit_grads",
    )(returned.reshape(all_rows, feat), tokens, turned, dispatch, part_comb)

    pieces = exchange(router_term)
    through_slots = jnp.einsum("bmn,bnd->bmd", weights, slot_in_grad, preferred_element_type=f32)
    through_router = jnp.einsum("bmn,dn->bmd", grad_logits, router, preferred_element_type=f32)
    grad_tokens = (through_slots + through_router).astype(bf16)
    grad_router = jnp.sum(pieces.astype(f32) * (1.0 / (images * devs)), axis=0)
    return (grad_tokens, grad_router)


def solution(mesh):
    in_specs = (
        P(("expert", "hidden"), None, None),
        P(),
        P(("expert", "hidden"), None, None),
        P(("expert", "hidden"), None, None),
        P("expert", None, "hidden"),
        P("expert", None, "hidden"),
        P("expert", "hidden", None),
    )
    out_specs = (P(("expert", "hidden"), None, None), P(("expert", "hidden"), None))
    return jax.shard_map(shards, mesh=mesh, in_specs=in_specs, out_specs=out_specs, check_vma=False)
```
